32 devices in a mesh: row: 8 (over y, x, core), col: 4 (over z).
Axes of the slice: x: 2, y: 2, z: 4, core: 2. Of those that a mesh axis runs over, the one named last changes fastest.
Arguments:
- start_vectors: bfloat16 [16384, 128], P(('row', 'col')), may hold values from -6 to 6
- tiles: bfloat16 [8, 128, 128, 128], P('row', 'col'), may hold values from -0.09375 to 0.09375
- tile_rows: int32 [8, 128], P('row', 'col'), may hold values from 0 to 15, as said below
- tile_cols: int32 [8, 128], P('row', 'col'), may hold values from 0 to 19
- tile_counts: int32 [8, 4], P('row', 'col'), may hold values from 4 to 32, as said below
- center: float32 [1], replicated, may hold values from -1 to 1
- half_width: float32 [1], replicated, may hold values from 2 to 3
Outputs:
- filtered: bfloat16 [16384, 128], P(('row', 'col'))
The draws below stay inside these ranges and needn't reach their ends.
Inputs may be any that keep to these rules, and one draw needn't show every extreme that they name: On each device the 32 slots name different places (tile_rows, tile_cols); only the first tile_counts slots are in use. `tile_counts`: some device uses exactly 32 slots.
All inputs are finite; a program needn't handle non-finite values.
Results may differ from the reference program's by a relative error of at most 0.009.
Values may be sent and summed in bfloat16 or wider, within the bound.
A program may use at most 64 MiB of HBM per device.

```python
import jax
import jax.numpy as jnp
from jax import lax

SEG = 2048
TILE = 128
NV = 128
MAXT = 32
NSEG = 8
PIECES = 4
BLOCKS = 5
TROWS = 16
TCOLS = 4
STATES = 16384
SLOTS = 128


def tile_layout(key):
    base_key = jax.random.fold_in(key, 7321)
    key_list = jax.random.split(base_key, NSEG * PIECES)

    def one_device(device_key):
        return jax.random.permutation(device_key, TROWS * BLOCKS * TCOLS)[:MAXT]
    places = jax.vmap(one_device)(key_list)
    return places.reshape(NSEG, PIECES * MAXT).astype(jnp.int32)


def draw_tile_rows(key, part):
    return (tile_layout(key) // (BLOCKS * TCOLS)).astype(jnp.int32)


def draw_tile_cols(key, part):
    return (tile_layout(key) % (BLOCKS * TCOLS)).astype(jnp.int32)


def draw_tile_counts(key, part):
    base_key = jax.random.fold_in(key, 9157)
    level_key, full_key = jax.random.split(base_key)
    lowest = max(MAXT // 8, 1)
    level_draw = jax.random.randint(level_key, (NSEG * PIECES,), 0, 64)
    counts = lowest + (MAXT - lowest) * level_draw * level_draw // 3969
    fullest = jax.random.randint(full_key, (), 0, NSEG * PIECES)
    counts = jnp.where(jnp.arange(NSEG * PIECES) == fullest, MAXT, counts)
    return counts.reshape(NSEG, PIECES).astype(jnp.int32)


def block_levels(own_key, dims, pieces, least, high):
    gain, own = 1.0, jax.random.fold_in(own_key, 6)
    for dim, parts in pieces:
        heights = jnp.exp(jax.random.uniform(jax.random.fold_in(own, dim), (parts,), jnp.float32, least / len(pieces), high / len(pieces)))
        gain = gain * jnp.repeat(heights, dims[dim] // parts).reshape([-1 if axis == dim else 1 for axis in range(len(dims))])
    return gain


def bell_draw(stream_key, shape, scale, bound, cuts=(), kind=jnp.bfloat16):
    values = scale * jax.random.normal(stream_key, shape, jnp.float32)
    if cuts:
        values = values * block_levels(stream_key, shape, cuts, -0.22, 0.18)
    return jnp.clip(values, -bound, bound).astype(kind)


def setup_inputs(seed: int = 0) -> dict:
    streams_of = jax.random.split(jax.random.key(seed), 8)
    return {
        "start_vectors": bell_draw(streams_of[0], (STATES, NV), 1.0, 6.0, ((0, 32),)),
        "tiles": bell_draw(streams_of[1], (NSEG, SLOTS, TILE, TILE), (MAXT * TILE) ** -0.5, 0.09375, ((0, 8), (1, 4))),
        "tile_rows": draw_tile_rows(jax.random.fold_in(streams_of[7], 71), 0),
        "tile_cols": draw_tile_cols(jax.random.fold_in(streams_of[7], 71), 0),
        "tile_counts": draw_tile_counts(jax.random.fold_in(streams_of[7], 71), 0),
        "center": jnp.clip(jax.random.uniform(streams_of[5], (1,), jnp.float32, -1.0, 1.0), -1.0, 1.0),
        "half_width": jnp.clip(jax.random.uniform(streams_of[6], (1,), jnp.float32, 2.0, 3.0), 2.0, 3.0),
    }


def apply_operator(vectors, tiles, tile_rows, tile_cols, tile_counts):
    segments = vectors.reshape(NSEG, TROWS, TILE, NV)
    zero_index = jnp.zeros((), jnp.int32)

    def one_device(totals, device_index):
        direct_sum, back_sum = totals
        seg_row = (device_index // PIECES).astype(jnp.int32)
        piece_index = (device_index % PIECES).astype(jnp.int32)
        slot_start = (piece_index * MAXT).astype(jnp.int32)
        tile_block = lax.dynamic_slice(tiles, (seg_row, slot_start, zero_index, zero_index), (1, MAXT, TILE, TILE))[0]
        rows_list = lax.dynamic_slice(tile_rows, (seg_row, slot_start), (1, MAXT))[0]
        cols_list = lax.dynamic_slice(tile_cols, (seg_row, slot_start), (1, MAXT))[0]
        live_count = lax.dynamic_slice(tile_counts, (seg_row, piece_index), (1, 1))[0, 0]
        in_use = (jnp.arange(MAXT, dtype=jnp.int32) < live_count).astype(jnp.float32)
        seg_col = ((seg_row + cols_list // TCOLS) % NSEG).astype(jnp.int32)
        tile_col = (piece_index * TCOLS + cols_list % TCOLS).astype(jnp.int32)
        tile_float = tile_block.astype(jnp.float32)
        inputs = segments[seg_col, tile_col].astype(jnp.float32)
        forward = jnp.einsum("tab,tbn->tan", tile_float, inputs, precision=lax.Precision.HIGHEST) * in_use[:, None, None]
        direct_sum = direct_sum.at[seg_row, rows_list].add(forward)
        own_rows = segments[seg_row, rows_list].astype(jnp.float32)
        backward = jnp.einsum("tab,tan->tbn", tile_float, own_rows, precision=lax.Precision.HIGHEST) * in_use[:, None, None]
        back_sum = back_sum.at[seg_col, tile_col].add(backward)
        return (direct_sum, back_sum), None

    empty_sum = jnp.zeros((NSEG, TROWS, TILE, NV), jnp.float32)
    totals, unused = lax.scan(one_device, (empty_sum, empty_sum), jnp.arange(NSEG * PIECES, dtype=jnp.int32))
    return (totals[0] + totals[1]).reshape(NSEG * SEG, NV)


def reference(start_vectors, tiles, tile_rows, tile_cols, tile_counts, center, half_width):
    shift_value = center[0]
    width_value = half_width[0]
    start_float = start_vectors.astype(jnp.float32)
    applied = apply_operator(start_vectors, tiles, tile_rows, tile_cols, tile_counts)
    first_step = ((applied - shift_value * start_float) / width_value).astype(jnp.bfloat16)
    applied = apply_operator(first_step, tiles, tile_rows, tile_cols, tile_counts)
    filtered = 2.0 * (applied - shift_value * first_step.astype(jnp.float32)) / width_value - start_float
    return filtered.astype(jnp.bfloat16)
```

```python
import functools

import jax
import jax.numpy as jnp
from jax import lax
from jax.experimental import pallas as pl
from jax.experimental.pallas import tpu as pltpu
from jax.sharding import PartitionSpec as P

CHUNKS = 2
UNROLL = 8
MESH_ID = pl.DeviceIdType.MESH


def link_slots(rows_ref, cols_ref, counts_ref, prev_ref, last_ref, *, slots, row_tiles, col_tiles):
    for side, (keys, size) in enumerate(((rows_ref, row_tiles), (cols_ref, col_tiles))):
        for k in range(size):
            last_ref[side, k] = slots
        for s in range(slots):
            key = keys[0, s]
            used = s < counts_ref[0, 0]
            before = last_ref[side, key]
            prev_ref[side, s] = jnp.where(used, before, slots)
            last_ref[side, key] = jnp.where(used, s, before)


def filter_kernel(
    dims, x_ref, tiles_ref, rows_ref, cols_ref, prev_ref, last_ref, center_ref, width_ref,
    out_ref, *scratch,
):
    R, C, half, pt, slots, vec, size = dims
    vc = vec // CHUNKS
    it = iter(scratch)
    win = [[next(it) for _ in range(CHUNKS)] for _ in range(2)]
    seg = [[next(it) for _ in range(CHUNKS)] for _ in range(2)]
    row_out = [[next(it) for _ in range(CHUNKS)] for _ in range(2)]
    col_out = [[next(it) for _ in range(CHUNKS)] for _ in range(2)]
    row_in = [[next(it) for _ in range(CHUNKS)] for _ in range(2)]
    col_in = [[next(it) for _ in range(CHUNKS)] for _ in range(2)]
    back = [next(it) for _ in range(CHUNKS)]
    direct = [next(it) for _ in range(CHUNKS)]
    result = next(it)
    row_send, row_recv, col_send, col_recv = (next(it) for _ in range(4))

    r = lax.axis_index("row")
    c = lax.axis_index("col")

    row_offsets = sorted({b % R for b in range(1, half + 1)} | {-b % R for b in range(1, half + 1)})
    barrier = pltpu.get_barrier_semaphore()
    for off in row_offsets:
        pl.semaphore_signal(barrier, inc=1, device_id={"row": lax.rem(r + off, R)}, device_id_type=MESH_ID)
    for off in range(1, C):
        pl.semaphore_signal(barrier, inc=1, device_id={"col": lax.rem(c + off, C)}, device_id_type=MESH_ID)

    for j in range(pt):
        block = x_ref[j * size:(j + 1) * size, :].astype(jnp.float32).T.astype(jnp.bfloat16)
        for h in range(CHUNKS):
            part = block[h * vc:(h + 1) * vc, :]
            win[0][h][j] = part
            seg[0][h][c * pt + j] = part
    for h in range(CHUNKS):
        back[h][slots] = jnp.zeros((vc, size), jnp.float32)
        direct[h][slots] = jnp.zeros((vc, size), jnp.float32)
    pl.semaphore_wait(barrier, len(row_offsets) + C - 1)

    def gather_copies(t, h):
        own = win[t][h].at[pl.ds(0, pt)]
        cols = [
            pltpu.make_async_remote_copy(
                src_ref=own, dst_ref=seg[t][h].at[pl.ds(c * pt, pt)],
                send_sem=col_send.at[t, h, 0, d], recv_sem=col_recv.at[t, h, 0, d],
                device_id={"col": lax.rem(c + d, C)}, device_id_type=MESH_ID)
            for d in range(1, C)
        ]
        rows = [
            pltpu.make_async_remote_copy(
                src_ref=own, dst_ref=win[t][h].at[pl.ds(b * pt, pt)],
                send_sem=row_send.at[t, h, 0, b], recv_sem=row_recv.at[t, h, 0, b],
                device_id={"row": lax.rem(r + R - b, R)}, device_id_type=MESH_ID)
            for b in range(1, half + 1)
        ]
        return cols, rows

    def row_returns(t, h):
        return [
            pltpu.make_async_remote_copy(
                src_ref=row_out[t][h].at[b - 1], dst_ref=row_in[t][h].at[b - 1],
                send_sem=row_send.at[t, h, 1, b], recv_sem=row_recv.at[t, h, 1, b],
                device_id={"row": lax.rem(r + b, R)}, device_id_type=MESH_ID)
            for b in range(1, half + 1)
        ]

    def col_returns(t, h):
        return [
            pltpu.make_async_remote_copy(
                src_ref=col_out[t][h].at[d - 1], dst_ref=col_in[t][h].at[d - 1],
                send_sem=col_send.at[t, h, 1, d], recv_sem=col_recv.at[t, h, 1, d],
                device_id={"col": lax.rem(c + d, C)}, device_id_type=MESH_ID)
            for d in range(1, C)
        ]

    started = []

    def start_all(copies):
        for copy in copies:
            copy.start()
        started.extend(copies)
        return copies

    def products(source, index_ref, side, sums, transposed):
        contract = (((1,), (0,)), ((), ())) if transposed else (((1,), (1,)), ((), ()))

        def one(s, carry):
            term = lax.dot_general(
                source[index_ref[0, s]], tiles_ref[0, s], contract,
                preferred_element_type=jnp.float32)
            sums[s] = sums[prev_ref[side, s]] + term
            return carry

        lax.fori_loop(0, slots, one, 0, unroll=UNROLL)

    def compute(t, h, copies):
        cols, rows = copies
        for copy in cols:
            copy.wait_recv()
        products(seg[t][h], rows_ref, 1, back[h], True)
        for b in range(1, half + 1):
            for j in range(pt):
                row_out[t][h][b - 1, j] = back[h][last_ref[1, b * pt + j]].astype(jnp.bfloat16)
        returns = start_all(row_returns(t, h))
        for copy in rows:
            copy.wait_recv()
        products(win[t][h], cols_ref, 0, direct[h], False)
        for d in range(1, C):
            piece = lax.rem(c + d, C)
            for j in range(pt):
                col_out[t][h][d - 1, j] = direct[h][last_ref[0, piece * pt + j]].astype(jnp.bfloat16)
        return returns, start_all(col_returns(t, h))

    def applied(t, h, returns, j):
        total = back[h][last_ref[1, j]] + direct[h][last_ref[0, c * pt + j]]
        for b in range(half):
            total += row_in[t][h][b, j].astype(jnp.float32)
        for d in range(C - 1):
            total += col_in[t][h][d, j].astype(jnp.float32)
        return total

    shift = center_ref[0]
    width = width_ref[0]
    gathers = [None] * CHUNKS
    for h in range(CHUNKS):
        cols, rows = gather_copies(0, h)
        gathers[h] = (start_all(cols), start_all(rows))
    for t in range(2):
        returns = [compute(t, h, gathers[h]) for h in range(CHUNKS)]
        for h in range(CHUNKS):
            for group in returns[h]:
                for copy in group:
                    copy.wait_recv()
            for j in range(pt):
                begin = win[0][h][j].astype(jnp.float32)
                if t == 0:
                    first = ((applied(t, h, returns, j) - shift * begin) / width).astype(jnp.bfloat16)
                    win[1][h][j] = first
                    seg[1][h][c * pt + j] = first
                else:
                    first = win[1][h][j].astype(jnp.float32)
                    value = 2.0 * (applied(t, h, returns, j) - shift * first) / width - begin
                    result[j, h * vc:(h + 1) * vc, :] = value
            if t == 0:
                cols, rows = gather_copies(1, h)
                gathers[h] = (start_all(cols), start_all(rows))
    for j in range(pt):
        out_ref[j * size:(j + 1) * size, :] = result[j].T.astype(jnp.bfloat16)
    for copy in started:
        copy.wait_send()


def per_device(start_vectors, tiles, tile_rows, tile_cols, tile_counts, center, half_width):
    R = lax.axis_size("row")
    C = lax.axis_size("col")
    half = R // 2
    piece_rows, vec = start_vectors.shape
    size = tiles.shape[-1]
    slots = tiles.shape[1]
    pt = piece_rows // size
    vc = vec // CHUNKS
    row_tiles = pt * C
    col_tiles = pt * (half + 1)
    smem = pl.BlockSpec(memory_space=pltpu.SMEM)
    vmem = pl.BlockSpec(memory_space=pltpu.VMEM)
    prev, last = pl.pallas_call(
        functools.partial(link_slots, slots=slots, row_tiles=row_tiles, col_tiles=col_tiles),
        out_shape=(
            jax.ShapeDtypeStruct((2, slots), jnp.int32),
            jax.ShapeDtypeStruct((2, max(row_tiles, col_tiles)), jnp.int32),
        ),
        in_specs=[smem] * 3,
        out_specs=(smem, smem),
        name="link_slots",
    )(tile_rows, tile_cols, tile_counts)

    bf, f32 = jnp.bfloat16, jnp.float32

    def pair(shape, dtype):
        return [pltpu.VMEM(shape, dtype) for _ in range(2 * CHUNKS)]

    scratch = (
        pair((col_tiles, vc, size), bf)
        + pair((row_tiles, vc, size), bf)
        + pair((half, pt, vc, size), bf)
        + pair((C - 1, pt, vc, size), bf)
        + pair((half, pt, vc, size), bf)
        + pair((C - 1, pt, vc, size), bf)
        + [pltpu.VMEM((slots + 1, vc, size), f32) for _ in range(2 * CHUNKS)]
        + [pltpu.VMEM((pt, vec, size), f32)]
        + [pltpu.SemaphoreType.DMA((2, CHUNKS, 2, half + 1))] * 2
        + [pltpu.SemaphoreType.DMA((2, CHUNKS, 2, C))] * 2
    )
    return pl.pallas_call(
        functools.partial(filter_kernel, (R, C, half, pt, slots, vec, size)),
        out_shape=jax.ShapeDtypeStruct((piece_rows, vec), bf),
        in_specs=[vmem, vmem, smem, smem, smem, smem, smem, smem],
        out_specs=vmem,
        scratch_shapes=scratch,
        compiler_params=pltpu.CompilerParams(
            collective_id=0, has_side_effects=True, vmem_limit_bytes=40 << 20),
        name="filter_steps",
    )(start_vectors, tiles, tile_rows, tile_cols, prev, last, center, half_width)


def solution(mesh):
    return jax.shard_map(
        per_device,
        mesh=mesh,
        in_specs=(
            P(("row", "col"), None),
            P("row", "col", None, None),
            P("row", "col"),
            P("row", "col"),
            P("row", "col"),
            P(),
            P(),
        ),
        out_specs=P(("row", "col"), None),
        check_vma=False,
    )
```

```python
import functools

import jax
import jax.numpy as jnp
from jax import lax
from jax.experimental import pallas as pl
from jax.experimental.pallas import tpu as pltpu
from jax.sharding import PartitionSpec as P

CHUNKS = 2
UNROLL = 8
MESH_ID = pl.DeviceIdType.MESH
ROW_AT, COL_AT, ROW_PREV, COL_PREV, ROW_LAST, COL_LAST = range(6)


def link_slots(rows_ref, cols_ref, counts_ref, table_ref, *, slots, pt, row_tiles, span):
    e = lax.rem(lax.axis_index("row"), 2)
    for k in range(row_tiles):
        table_ref[ROW_LAST, k] = slots
    for k in range(span):
        table_ref[COL_LAST, k] = slots
    for s in range(slots):
        used = s < counts_ref[0, 0]
        row = rows_ref[0, s]
        col = cols_ref[0, s] + e * pt
        table_ref[ROW_AT, s] = (row // pt * 2 + e) * pt + row % pt
        table_ref[COL_AT, s] = col
        for key, prev, last in ((row, ROW_PREV, ROW_LAST), (col, COL_PREV, COL_LAST)):
            before = table_ref[last, key]
            table_ref[prev, s] = jnp.where(used, before, slots)
            table_ref[last, key] = jnp.where(used, s, before)


def filter_kernel(dims, x_ref, tiles_ref, table_ref, center_ref, width_ref, out_ref, *scratch):
    R, C, hw, pt, slots, vec, size = dims
    vc = vec // 2 // CHUNKS
    unit = 2 * pt
    it = iter(scratch)

    def grid2():
        return [[next(it) for _ in range(CHUNKS)] for _ in range(2)]

    win, seg, row_out, row_in = grid2(), grid2(), grid2(), grid2()
    z_out = [grid2(), grid2()]
    z_in = [grid2(), grid2()]
    back, direct = grid2(), grid2()
    halves, final = next(it), next(it)
    tiles = [next(it), next(it)]
    tabs = [next(it), next(it)]
    tab_land = next(it)
    row_send, row_recv, z_send, z_recv, pair_send, pair_recv, local = (next(it) for _ in range(7))

    r = lax.axis_index("row")
    c = lax.axis_index("col")
    e = lax.rem(r, 2)
    partner = {"row": r + 1 - 2 * e}

    def chip_row(o):
        return {"row": lax.rem(r + 2 * o + R, R)}

    offsets = sorted({2 * o % R for o in range(1, hw + 1)} | {-2 * o % R for o in range(1, hw + 1)})
    barrier = pltpu.get_barrier_semaphore()
    for off in offsets:
        pl.semaphore_signal(barrier, inc=1, device_id={"row": lax.rem(r + off, R)}, device_id_type=MESH_ID)
    for off in (1, C - 1):
        pl.semaphore_signal(barrier, inc=1, device_id={"col": lax.rem(c + off, C)}, device_id_type=MESH_ID)
    pl.semaphore_signal(barrier, inc=1, device_id=partner, device_id_type=MESH_ID)

    own_tiles = pltpu.make_async_copy(tiles_ref.at[0], tiles[0], local.at[0])
    own_table = pltpu.make_async_copy(table_ref, tabs[0], local.at[1])
    own_tiles.start()
    own_table.start()
    for j in range(pt):
        block = x_ref[j * size:(j + 1) * size, :].astype(jnp.float32).T.astype(jnp.bfloat16)
        for a in range(2):
            for h in range(CHUNKS):
                at = (a * CHUNKS + h) * vc
                halves[a, h, j] = block[at:at + vc, :]
    for h in range(CHUNKS):
        for j in range(pt):
            win[0][h][e * pt + j] = halves[e, h, j]
        for side in range(2):
            back[side][h][slots] = jnp.zeros((vc, size), jnp.float32)
            direct[side][h][slots] = jnp.zeros((vc, size), jnp.float32)
    for way, edge in ((0, 0), (1, C - 1)):
        @pl.when(c == edge)
        def _():
            for t in range(2):
                for h in range(CHUNKS):
                    z_in[way][t][h][...] = jnp.zeros((C - 1, unit, vc, size), jnp.bfloat16)
    pl.semaphore_wait(barrier, len(offsets) + 3)

    drains = []

    def remote(src, dst, send, recv, device):
        return pltpu.make_async_remote_copy(
            src_ref=src, dst_ref=dst, send_sem=send, recv_sem=recv,
            device_id=device, device_id_type=MESH_ID)

    def start(copy, valid=None):
        if valid is None:
            copy.start()
        else:
            pl.when(valid)(copy.start)
        drains.append((copy, valid))
        return copy

    def step_wait(copy, valid):
        pl.when(valid)(copy.wait_recv)

    swap = [
        start(remote(halves.at[1 - e, h], win[0][h].at[pl.ds(e * pt, pt)],
                     pair_send.at[h], pair_recv.at[h], partner))
        for h in range(CHUNKS)
    ]
    pair_table = start(remote(table_ref, tab_land, pair_send.at[CHUNKS], pair_recv.at[CHUNKS], partner))
    pair_tiles = start(remote(tiles_ref.at[0], tiles[1], pair_send.at[CHUNKS + 1], pair_recv.at[CHUNKS + 1], partner))

    def has_from(way, d):
        return c - d >= 0 if way == 0 else c + d < C

    def has_to(way, d):
        return has_from(1 - way, d)

    def onward(way):
        return {"col": lax.rem(c + (1 if way == 0 else C - 1), C)}

    def z_gather(t, h, way, d):
        origin = lax.rem(c + (C - d if way == 0 else d), C)
        place = seg[t][h].at[pl.ds(origin * unit, unit)]
        return remote(win[t][h].at[pl.ds(0, unit)] if d == 0 else place, place,
                      z_send.at[t, h, 0, way, d], z_recv.at[t, h, 0, way, d], onward(way))

    def start_gather(t, h):
        for j in range(unit):
            seg[t][h][c * unit + j] = win[t][h][j]
        for way in range(2):
            start(z_gather(t, h, way, 0), has_to(way, 1))
        return [
            start(remote(win[t][h].at[pl.ds(0, unit)], win[t][h].at[pl.ds(o * unit, unit)],
                         row_send.at[t, h, 0, o], row_recv.at[t, h, 0, o], chip_row(-o)))
            for o in range(1, hw + 1)
        ]

    def relay(t, h):
        for d in range(1, C):
            for way in range(2):
                place = lax.rem(c + (C - d if way == 0 else d), C)
                view = seg[t][h].at[pl.ds(place * unit, unit)]
                landed = remote(view, view, z_send.at[t, h, 0, way, d - 1],
                                z_recv.at[t, h, 0, way, d - 1], onward(way))
                step_wait(landed, has_from(way, d))
                if d < C - 1:
                    start(z_gather(t, h, way, d), has_from(way, d) & has_to(way, 1))

    def products(source, side, h, transposed):
        at, prev = (ROW_AT, COL_PREV) if transposed else (COL_AT, ROW_PREV)
        sums = (back if transposed else direct)[side][h]
        contract = (((1,), (0,)), ((), ())) if transposed else (((1,), (1,)), ((), ()))

        def one(s, carry):
            term = lax.dot_general(
                source[tabs[side][at, s]], tiles[side][s], contract,
                preferred_element_type=jnp.float32)
            sums[s] = sums[tabs[side][prev, s]] + term
            return carry

        lax.fori_loop(0, slots, one, 0, unroll=UNROLL)

    def back_sum(h, place):
        return (back[0][h][tabs[0][COL_LAST, place]] + back[1][h][tabs[1][COL_LAST, place]])

    def back_products(t, h):
        for side in range(2):
            products(seg[t][h], side, h, True)
        for o in range(1, hw + 1):
            for m in range(unit):
                row_out[t][h][o - 1, m] = back_sum(h, o * unit + m).astype(jnp.bfloat16)
        return [
            start(remote(row_out[t][h].at[o - 1], row_in[t][h].at[o - 1],
                         row_send.at[t, h, 1, o], row_recv.at[t, h, 1, o], chip_row(o)))
            for o in range(1, hw + 1)
        ]

    def direct_products(t, h, arriving):
        for copy in arriving:
            copy.wait_recv()
        for side in range(2):
            products(win[t][h], side, h, False)

    def landing(t, h, way, d):
        return remote(z_out[way][t][h].at[d], z_in[way][t][h].at[d],
                      z_send.at[t, h, 1, way, d], z_recv.at[t, h, 1, way, d], onward(way))

    def chain(t, h, d):
        for way in range(2):
            step_wait(landing(t, h, way, d), has_from(way, 1) & has_to(way, d)) if d < C - 1 else None

            @pl.when(has_to(way, d))
            def _():
                piece = lax.rem(c + (d if way == 0 else C - d), C)
                for side in range(2):
                    parity = e if side == 0 else 1 - e
                    for j in range(pt):
                        value = direct[side][h][tabs[side][ROW_LAST, piece * pt + j]]
                        if d < C - 1:
                            value += z_in[way][t][h][d, parity * pt + j].astype(jnp.float32)
                        z_out[way][t][h][d - 1, parity * pt + j] = value.astype(jnp.bfloat16)

            start(landing(t, h, way, d - 1), has_to(way, d))

    def combine(t, h, returning):
        for copy in returning:
            copy.wait_recv()
        for way in range(2):
            step_wait(landing(t, h, way, 0), has_from(way, 1))
        shift = center_ref[0]
        width = width_ref[0]
        for side in range(2):
            parity = e if side == 0 else 1 - e
            for j in range(pt):
                m = parity * pt + j
                total = back_sum(h, m) + direct[side][h][tabs[side][ROW_LAST, c * pt + j]]
                for o in range(hw):
                    total += row_in[t][h][o, m].astype(jnp.float32)
                for way in range(2):
                    total += z_in[way][t][h][0, m].astype(jnp.float32)
                begin = win[0][h][m].astype(jnp.float32)
                if t == 0:
                    win[1][h][m] = ((total - shift * begin) / width).astype(jnp.bfloat16)
                else:
                    first = win[1][h][m].astype(jnp.float32)
                    value = (2.0 * (total - shift * first) / width - begin).astype(jnp.bfloat16)
                    if side == 0:
                        final[e, h, j] = value
                    else:
                        halves[e, h, j] = value

    arriving = [None] * CHUNKS
    for h in range(CHUNKS):
        swap[h].wait_recv()
        arriving[h] = start_gather(0, h)
    own_table.wait()
    pair_table.wait_recv()
    other_table = pltpu.make_async_copy(tab_land, tabs[1], local.at[2])
    other_table.start()
    other_table.wait()
    own_tiles.wait()
    pair_tiles.wait_recv()
    for copy in swap:
        copy.wait_send()
        drains.remove((copy, None))
    for t in range(2):
        returning = [None] * CHUNKS
        steps = []
        relay(t, 0)
        for h in range(CHUNKS):
            returning[h] = back_products(t, h)
            if h + 1 < CHUNKS:
                relay(t, h + 1)
            if h:
                for d in range(C - 2, 0, -1):
                    chain(t, h - 1, d)
            direct_products(t, h, arriving[h])
            chain(t, h, C - 1)
        for h in range(CHUNKS):
            if h == CHUNKS - 1:
                for d in range(C - 2, 0, -1):
                    chain(t, h, d)
            combine(t, h, returning[h])
            if t == 0:
                arriving[h] = start_gather(1, h)
            else:
                steps.append(start(remote(
                    halves.at[e, h], final.at[e, h], pair_send.at[CHUNKS + 2 + h],
                    pair_recv.at[CHUNKS + 2 + h], partner)))
    for copy in steps:
        copy.wait_recv()
    for j in range(pt):
        whole = jnp.concatenate(
            [final[a, h, j].astype(jnp.float32) for a in range(2) for h in range(CHUNKS)], axis=0)
        out_ref[j * size:(j + 1) * size, :] = whole.T.astype(jnp.bfloat16)
    for copy, valid in drains:
        if valid is None:
            copy.wait_send()
        else:
            pl.when(valid)(copy.wait_send)


def per_device(start_vectors, tiles, tile_rows, tile_cols, tile_counts, center, half_width):
    R = lax.axis_size("row")
    C = lax.axis_size("col")
    half = R // 2
    hw = half // 2
    piece_rows, vec = start_vectors.shape
    size = tiles.shape[-1]
    slots = tiles.shape[1]
    pt = piece_rows // size
    vc = vec // 2 // CHUNKS
    unit = 2 * pt
    row_tiles = pt * C
    span = pt * (half + 2)
    lanes = pl.cdiv(max(slots, row_tiles, span), 128) * 128
    smem = pl.BlockSpec(memory_space=pltpu.SMEM)
    vmem = pl.BlockSpec(memory_space=pltpu.VMEM)
    anywhere = pl.BlockSpec(memory_space=pl.ANY)
    table = pl.pallas_call(
        functools.partial(link_slots, slots=slots, pt=pt, row_tiles=row_tiles, span=span),
        out_shape=jax.ShapeDtypeStruct((8, lanes), jnp.int32),
        in_specs=[smem] * 3,
        out_specs=smem,
        name="link_slots",
    )(tile_rows, tile_cols, tile_counts)

    bf, f32 = jnp.bfloat16, jnp.float32

    def pair(shape, dtype):
        return [pltpu.VMEM(shape, dtype) for _ in range(2 * CHUNKS)]

    scratch = (
        pair(((hw + 1) * unit, vc, size), bf)
        + pair((C * unit, vc, size), bf)
        + pair((hw, unit, vc, size), bf)
        + pair((hw, unit, vc, size), bf)
        + pair((C - 1, unit, vc, size), bf) * 2
        + pair((C - 1, unit, vc, size), bf) * 2
        + pair((slots + 1, vc, size), f32) * 2
        + [pltpu.VMEM((2, CHUNKS, pt, vc, size), bf)] * 2
        + [pltpu.VMEM((slots, size, size), bf)] * 2
        + [pltpu.SMEM((8, lanes), jnp.int32)] * 2
        + [pltpu.VMEM((8, lanes), jnp.int32)]
        + [pltpu.SemaphoreType.DMA((2, CHUNKS, 2, hw + 1))] * 2
        + [pltpu.SemaphoreType.DMA((2, CHUNKS, 2, 2, C))] * 2
        + [pltpu.SemaphoreType.DMA((2 * CHUNKS + 2,))] * 2
        + [pltpu.SemaphoreType.DMA((3,))]
    )
    return pl.pallas_call(
        functools.partial(filter_kernel, (R, C, hw, pt, slots, vec, size)),
        out_shape=jax.ShapeDtypeStruct((piece_rows, vec), bf),
        in_specs=[vmem, anywhere, anywhere, smem, smem],
        out_specs=vmem,
        scratch_shapes=scratch,
        compiler_params=pltpu.CompilerParams(
            collective_id=0, has_side_effects=True, vmem_limit_bytes=40 << 20),
        name="filter_steps",
    )(start_vectors, tiles, table, center, half_width)


def solution(mesh):
    return jax.shard_map(
        per_device,
        mesh=mesh,
        in_specs=(
            P(("row", "col"), None),
            P("row", "col", None, None),
            P("row", "col"),
            P("row", "col"),
            P("row", "col"),
            P(),
            P(),
        ),
        out_specs=P(("row", "col"), None),
        check_vma=False,
    )
```

```python
import functools

import jax
import jax.numpy as jnp
from jax import lax
from jax.experimental import pallas as pl
from jax.experimental.pallas import tpu as pltpu
from jax.sharding import PartitionSpec as P

CHUNKS = 2
UNROLL = 8
MESH_ID = pl.DeviceIdType.MESH
ROW_AT, COL_AT, ROW_PREV, COL_PREV, ROW_LAST, COL_LAST = range(6)


def link_slots(rows_ref, cols_ref, counts_ref, table_ref, *, slots, pt, row_tiles, span):
    e = lax.rem(lax.axis_index("row"), 2)
    for k in range(row_tiles):
        table_ref[ROW_LAST, k] = slots
    for k in range(span):
        table_ref[COL_LAST, k] = slots
    for s in range(slots):
        used = s < counts_ref[0, 0]
        row = rows_ref[0, s]
        col = cols_ref[0, s] + e * pt
        table_ref[ROW_AT, s] = (row // pt * 2 + e) * pt + row % pt
        table_ref[COL_AT, s] = col
        for key, prev, last in ((row, ROW_PREV, ROW_LAST), (col, COL_PREV, COL_LAST)):
            before = table_ref[last, key]
            table_ref[prev, s] = jnp.where(used, before, slots)
            table_ref[last, key] = jnp.where(used, s, before)


def filter_kernel(dims, x_ref, tiles_ref, table_ref, center_ref, width_ref, out_ref, *scratch):
    R, C, hw, pt, slots, vec, size = dims
    vc = vec // 2 // CHUNKS
    unit = 2 * pt
    it = iter(scratch)

    def grid2():
        return [[next(it) for _ in range(CHUNKS)] for _ in range(2)]

    win, seg, row_out, row_in = grid2(), grid2(), grid2(), grid2()
    z_out, z_in, z_mid = grid2(), grid2(), grid2()
    back, direct = grid2(), grid2()
    halves, final = next(it), next(it)
    tiles = [next(it), next(it)]
    tabs = [next(it), next(it)]
    tab_land = next(it)
    row_send, row_recv, z_send, z_recv, pair_send, pair_recv, local = (next(it) for _ in range(7))

    r = lax.axis_index("row")
    c = lax.axis_index("col")
    e = lax.rem(r, 2)
    partner = {"row": r + 1 - 2 * e}

    def chip_row(o):
        return {"row": lax.rem(r + 2 * o + R, R)}

    offsets = sorted({2 * o % R for o in range(1, hw + 1)} | {-2 * o % R for o in range(1, hw + 1)})
    barrier = pltpu.get_barrier_semaphore()
    for off in offsets:
        pl.semaphore_signal(barrier, inc=1, device_id={"row": lax.rem(r + off, R)}, device_id_type=MESH_ID)
    for off in range(1, C):
        pl.semaphore_signal(barrier, inc=1, device_id={"col": lax.rem(c + off, C)}, device_id_type=MESH_ID)
    pl.semaphore_signal(barrier, inc=1, device_id=partner, device_id_type=MESH_ID)

    own_tiles = pltpu.make_async_copy(tiles_ref.at[0], tiles[0], local.at[0])
    own_table = pltpu.make_async_copy(table_ref, tabs[0], local.at[1])
    own_tiles.start()
    own_table.start()
    for j in range(pt):
        block = x_ref[j * size:(j + 1) * size, :].astype(jnp.float32).T.astype(jnp.bfloat16)
        for a in range(2):
            for h in range(CHUNKS):
                at = (a * CHUNKS + h) * vc
                halves[a, h, j] = block[at:at + vc, :]
    for h in range(CHUNKS):
        for j in range(pt):
            win[0][h][e * pt + j] = halves[e, h, j]
        for side in range(2):
            back[side][h][slots] = jnp.zeros((vc, size), jnp.float32)
            direct[side][h][slots] = jnp.zeros((vc, size), jnp.float32)
    first_end, last_end = c == 0, c == C - 1
    inner = jnp.logical_not(first_end | last_end)

    def gives_to(d):
        to = lax.rem(c + d, C)
        to_inner = (to > 0) & (to < C - 1)
        return to_inner | ((to == 0) & (c == 1)) | ((to == C - 1) & (c == C - 2))

    def takes_from(d):
        source = lax.rem(c + d, C)
        return (((source > 0) & (source < C - 1)) | ((source == 0) & (c == 1))
                | ((source == C - 1) & (c == C - 2)))

    def helps(end, d):
        other = lax.rem(c + d, C)
        return (c == 1) & (other >= 2) if end == 0 else (c == C - 2) & (other <= C - 3)

    for d in range(1, C):
        @pl.when(jnp.logical_not(takes_from(d)))
        def _():
            for t in range(2):
                for h in range(CHUNKS):
                    z_in[t][h][d - 1] = jnp.zeros((unit, vc, size), jnp.bfloat16)
    pl.semaphore_wait(barrier, len(offsets) + C)

    drains = []

    def remote(src, dst, send, recv, device):
        return pltpu.make_async_remote_copy(
            src_ref=src, dst_ref=dst, send_sem=send, recv_sem=recv,
            device_id=device, device_id_type=MESH_ID)

    def start(copy, valid=None):
        if valid is None:
            copy.start()
        else:
            pl.when(valid)(copy.start)
        drains.append((copy, valid))
        return copy

    def step_wait(copy, valid):
        pl.when(valid)(copy.wait_recv)

    swap = [
        start(remote(halves.at[1 - e, h], win[0][h].at[pl.ds(e * pt, pt)],
                     pair_send.at[h], pair_recv.at[h], partner))
        for h in range(CHUNKS)
    ]
    pair_table = start(remote(table_ref, tab_land, pair_send.at[CHUNKS], pair_recv.at[CHUNKS], partner))
    pair_tiles = start(remote(tiles_ref.at[0], tiles[1], pair_send.at[CHUNKS + 1], pair_recv.at[CHUNKS + 1], partner))

    near_first = sorted(range(1, C), key=lambda d: min(d, C - d))

    def z_unit(t, h, origin):
        return seg[t][h].at[pl.ds(origin * unit, unit)]

    def z_gather(t, h, d):
        return remote(win[t][h].at[pl.ds(0, unit)], z_unit(t, h, c),
                      z_send.at[t, h, 0, d], z_recv.at[t, h, 0, C - d],
                      {"col": lax.rem(c + d, C)})

    def z_forward(t, h, end, d):
        view = z_unit(t, h, lax.rem(c + d, C))
        slot = (1 + d) % C if end == 0 else d - 1
        return remote(view, view, z_send.at[t, h, 1 + end, d], z_recv.at[t, h, 0, slot],
                      {"col": lax.rem(c + (C - 1 if end == 0 else 1), C)})

    def start_gather(t, h):
        for j in range(unit):
            seg[t][h][c * unit + j] = win[t][h][j]
        for d in reversed(near_first):
            start(z_gather(t, h, d), gives_to(d))
        return [
            start(remote(win[t][h].at[pl.ds(0, unit)], win[t][h].at[pl.ds(o * unit, unit)],
                         row_send.at[t, h, 0, o], row_recv.at[t, h, 0, o], chip_row(-o)))
            for o in range(1, hw + 1)
        ]

    def relay(t, h):
        for d in near_first:
            view = z_unit(t, h, lax.rem(c + d, C))
            remote(view, view, z_send.at[t, h, 0, d], z_recv.at[t, h, 0, d],
                   {"col": lax.rem(c + d, C)}).wait_recv()
            for end in range(2):
                if (1 + d if end == 0 else d - 1) % C:
                    start(z_forward(t, h, end, d), helps(end, d))

    def products(source, side, h, transposed):
        at, prev = (ROW_AT, COL_PREV) if transposed else (COL_AT, ROW_PREV)
        sums = (back if transposed else direct)[side][h]
        contract = (((1,), (0,)), ((), ())) if transposed else (((1,), (1,)), ((), ()))

        def one(s, carry):
            term = lax.dot_general(
                source[tabs[side][at, s]], tiles[side][s], contract,
                preferred_element_type=jnp.float32)
            sums[s] = sums[tabs[side][prev, s]] + term
            return carry

        lax.fori_loop(0, slots, one, 0, unroll=UNROLL)

    def back_sum(h, place):
        return (back[0][h][tabs[0][COL_LAST, place]] + back[1][h][tabs[1][COL_LAST, place]])

    def back_products(t, h):
        for side in range(2):
            products(seg[t][h], side, h, True)
        for o in range(1, hw + 1):
            for m in range(unit):
                row_out[t][h][o - 1, m] = back_sum(h, o * unit + m).astype(jnp.bfloat16)
        return [
            start(remote(row_out[t][h].at[o - 1], row_in[t][h].at[o - 1],
                         row_send.at[t, h, 1, o], row_recv.at[t, h, 1, o], chip_row(o)))
            for o in range(1, hw + 1)
        ]

    def direct_products(t, h, arriving):
        for copy in arriving:
            copy.wait_recv()
        for side in range(2):
            products(win[t][h], side, h, False)

    def z_sums(t, h, d, end=None):
        piece = lax.rem(c + d, C)
        for side in range(2):
            parity = e if side == 0 else 1 - e
            for j in range(pt):
                value = direct[side][h][tabs[side][ROW_LAST, piece * pt + j]]
                if end is not None:
                    value += z_mid[t][h][d - 1, parity * pt + j].astype(jnp.float32)
                z_out[t][h][d - 1, parity * pt + j] = value.astype(jnp.bfloat16)

    def z_return(t, h, d):
        return remote(z_out[t][h].at[d - 1], z_in[t][h].at[C - d - 1],
                      z_send.at[t, h, 3, d], z_recv.at[t, h, 1, C - d],
                      {"col": lax.rem(c + d, C)})

    def z_to_mid(t, h, end, d):
        slot = d - 1 if end == 0 else (d + 1) % C
        return remote(z_out[t][h].at[d - 1], z_mid[t][h].at[slot - 1],
                      z_send.at[t, h, 4 + end, d], z_recv.at[t, h, 2, slot],
                      {"col": lax.rem(c + (1 if end == 0 else C - 1), C)})

    def return_plain(t, h):
        for d in reversed(near_first):
            plain = jnp.logical_not(helps(0, d) | helps(1, d))

            @pl.when(plain)
            def _():
                z_sums(t, h, d)

            straight = inner
            if d == 1:
                straight = straight | first_end
            if d == C - 1:
                straight = straight | last_end
            start(z_return(t, h, d), straight & plain)
            if d >= 2:
                start(z_to_mid(t, h, 0, d), first_end)
            if d <= C - 2:
                start(z_to_mid(t, h, 1, d), last_end)

    def return_helped(t, h):
        for d in reversed(near_first):
            helped = helps(0, d) | helps(1, d)

            @pl.when(helped)
            def _():
                remote(z_out[t][h].at[d - 1], z_mid[t][h].at[d - 1], z_send.at[t, h, 3, d],
                       z_recv.at[t, h, 2, d], {"col": lax.rem(c + d, C)}).wait_recv()
                z_sums(t, h, d, 0)

            start(z_return(t, h, d), helped)

    def combine(t, h, returning):
        for copy in returning:
            copy.wait_recv()
        for d in range(1, C):
            step_wait(remote(z_out[t][h].at[d - 1], z_in[t][h].at[d - 1], z_send.at[t, h, 3, d],
                             z_recv.at[t, h, 1, d], {"col": lax.rem(c + d, C)}), takes_from(d))
        shift = center_ref[0]
        width = width_ref[0]
        for side in range(2):
            parity = e if side == 0 else 1 - e
            for j in range(pt):
                m = parity * pt + j
                total = back_sum(h, m) + direct[side][h][tabs[side][ROW_LAST, c * pt + j]]
                for o in range(hw):
                    total += row_in[t][h][o, m].astype(jnp.float32)
                for d in range(C - 1):
                    total += z_in[t][h][d, m].astype(jnp.float32)
                begin = win[0][h][m].astype(jnp.float32)
                if t == 0:
                    win[1][h][m] = ((total - shift * begin) / width).astype(jnp.bfloat16)
                else:
                    first = win[1][h][m].astype(jnp.float32)
                    value = (2.0 * (total - shift * first) / width - begin).astype(jnp.bfloat16)
                    if side == 0:
                        final[e, h, j] = value
                    else:
                        halves[e, h, j] = value

    arriving = [None] * CHUNKS
    for h in range(CHUNKS):
        swap[h].wait_recv()
        arriving[h] = start_gather(0, h)
    own_table.wait()
    pair_table.wait_recv()
    other_table = pltpu.make_async_copy(tab_land, tabs[1], local.at[2])
    other_table.start()
    other_table.wait()
    own_tiles.wait()
    pair_tiles.wait_recv()
    for copy in swap:
        copy.wait_send()
        drains.remove((copy, None))
    for t in range(2):
        returning = [None] * CHUNKS
        steps = []
        relay(t, 0)
        for h in range(CHUNKS):
            returning[h] = back_products(t, h)
            if h + 1 < CHUNKS:
                relay(t, h + 1)
            if h:
                return_helped(t, h - 1)
            direct_products(t, h, arriving[h])
            return_plain(t, h)
        return_helped(t, CHUNKS - 1)
        for h in range(CHUNKS):
            combine(t, h, returning[h])
            if t == 0:
                arriving[h] = start_gather(1, h)
            else:
                steps.append(start(remote(
                    halves.at[e, h], final.at[e, h], pair_send.at[CHUNKS + 2 + h],
                    pair_recv.at[CHUNKS + 2 + h], partner)))
    for copy in steps:
        copy.wait_recv()
    for j in range(pt):
        whole = jnp.concatenate(
            [final[a, h, j].astype(jnp.float32) for a in range(2) for h in range(CHUNKS)], axis=0)
        out_ref[j * size:(j + 1) * size, :] = whole.T.astype(jnp.bfloat16)
    for copy, valid in drains:
        if valid is None:
            copy.wait_send()
        else:
            pl.when(valid)(copy.wait_send)


def per_device(start_vectors, tiles, tile_rows, tile_cols, tile_counts, center, half_width):
    R = lax.axis_size("row")
    C = lax.axis_size("col")
    half = R // 2
    hw = half // 2
    piece_rows, vec = start_vectors.shape
    size = tiles.shape[-1]
    slots = tiles.shape[1]
    pt = piece_rows // size
    vc = vec // 2 // CHUNKS
    unit = 2 * pt
    row_tiles = pt * C
    span = pt * (half + 2)
    lanes = pl.cdiv(max(slots, row_tiles, span), 128) * 128
    smem = pl.BlockSpec(memory_space=pltpu.SMEM)
    vmem = pl.BlockSpec(memory_space=pltpu.VMEM)
    anywhere = pl.BlockSpec(memory_space=pl.ANY)
    table = pl.pallas_call(
        functools.partial(link_slots, slots=slots, pt=pt, row_tiles=row_tiles, span=span),
        out_shape=jax.ShapeDtypeStruct((8, lanes), jnp.int32),
        in_specs=[smem] * 3,
        out_specs=smem,
        name="link_slots",
    )(tile_rows, tile_cols, tile_counts)

    bf, f32 = jnp.bfloat16, jnp.float32

    def pair(shape, dtype):
        return [pltpu.VMEM(shape, dtype) for _ in range(2 * CHUNKS)]

    scratch = (
        pair(((hw + 1) * unit, vc, size), bf)
        + pair((C * unit, vc, size), bf)
        + pair((hw, unit, vc, size), bf)
        + pair((hw, unit, vc, size), bf)
        + pair((C - 1, unit, vc, size), bf) * 3
        + pair((slots + 1, vc, size), f32) * 2
        + [pltpu.VMEM((2, CHUNKS, pt, vc, size), bf)] * 2
        + [pltpu.VMEM((slots, size, size), bf)] * 2
        + [pltpu.SMEM((8, lanes), jnp.int32)] * 2
        + [pltpu.VMEM((8, lanes), jnp.int32)]
        + [pltpu.SemaphoreType.DMA((2, CHUNKS, 2, hw + 1))] * 2
        + [pltpu.SemaphoreType.DMA((2, CHUNKS, 6, C))] * 2
        + [pltpu.SemaphoreType.DMA((2 * CHUNKS + 2,))] * 2
        + [pltpu.SemaphoreType.DMA((3,))]
    )
    return pl.pallas_call(
        functools.partial(filter_kernel, (R, C, hw, pt, slots, vec, size)),
        out_shape=jax.ShapeDtypeStruct((piece_rows, vec), bf),
        in_specs=[vmem, anywhere, anywhere, smem, smem],
        out_specs=vmem,
        scratch_shapes=scratch,
        compiler_params=pltpu.CompilerParams(
            collective_id=0, has_side_effects=True, vmem_limit_bytes=40 << 20),
        name="filter_steps",
    )(start_vectors, tiles, table, center, half_width)


def solution(mesh):
    return jax.shard_map(
        per_device,
        mesh=mesh,
        in_specs=(
            P(("row", "col"), None),
            P("row", "col", None, None),
            P("row", "col"),
            P("row", "col"),
            P("row", "col"),
            P(),
            P(),
        ),
        out_specs=P(("row", "col"), None),
        check_vma=False,
    )
```

```python
import functools

import jax
import jax.numpy as jnp
from jax import lax
from jax.experimental import pallas as pl
from jax.experimental.pallas import tpu as pltpu
from jax.sharding import PartitionSpec as P

CHUNKS = 2
UNROLL = 8
MESH_ID = pl.DeviceIdType.MESH


def link_slots(rows_ref, cols_ref, counts_ref, prev_ref, last_ref, *, slots, row_tiles, col_tiles):
    for side, (keys, size) in enumerate(((rows_ref, row_tiles), (cols_ref, col_tiles))):
        for k in range(size):
            last_ref[side, k] = slots
        for s in range(slots):
            key = keys[0, s]
            used = s < counts_ref[0, 0]
            before = last_ref[side, key]
            prev_ref[side, s] = jnp.where(used, before, slots)
            last_ref[side, key] = jnp.where(used, s, before)


def filter_kernel(
    dims, x_ref, tiles_ref, rows_ref, cols_ref, prev_ref, last_ref, center_ref, width_ref,
    out_ref, *scratch,
):
    R, C, half, pt, slots, vec, size = dims
    vc = vec // CHUNKS
    it = iter(scratch)
    win = [[next(it) for _ in range(CHUNKS)] for _ in range(2)]
    seg = [[next(it) for _ in range(CHUNKS)] for _ in range(2)]
    row_out = [[next(it) for _ in range(CHUNKS)] for _ in range(2)]
    col_out = [[next(it) for _ in range(CHUNKS)] for _ in range(2)]
    row_in = [[next(it) for _ in range(CHUNKS)] for _ in range(2)]
    col_in = [[next(it) for _ in range(CHUNKS)] for _ in range(2)]
    back = [next(it) for _ in range(CHUNKS)]
    direct = [next(it) for _ in range(CHUNKS)]
    mid = [[next(it) for _ in range(CHUNKS)] for _ in range(2)]
    result = next(it)
    tiles, local = next(it), next(it)
    row_send, row_recv, col_send, col_recv = (next(it) for _ in range(4))

    r = lax.axis_index("row")
    c = lax.axis_index("col")

    row_offsets = sorted({b % R for b in range(1, half + 1)} | {-b % R for b in range(1, half + 1)})
    barrier = pltpu.get_barrier_semaphore()
    for off in row_offsets:
        pl.semaphore_signal(barrier, inc=1, device_id={"row": lax.rem(r + off, R)}, device_id_type=MESH_ID)
    for off in range(1, C):
        pl.semaphore_signal(barrier, inc=1, device_id={"col": lax.rem(c + off, C)}, device_id_type=MESH_ID)

    fetch = pltpu.make_async_copy(tiles_ref.at[0], tiles, local)
    fetch.start()
    for end, slot in ((0, 0), (C - 1, C - 2)):
        @pl.when(c == end)
        def _():
            for t in range(2):
                for h in range(CHUNKS):
                    col_in[t][h][slot] = jnp.zeros((pt, vc, size), jnp.bfloat16)
    for j in range(pt):
        block = x_ref[j * size:(j + 1) * size, :].astype(jnp.float32).T.astype(jnp.bfloat16)
        for h in range(CHUNKS):
            part = block[h * vc:(h + 1) * vc, :]
            win[0][h][j] = part
            seg[0][h][c * pt + j] = part
    for h in range(CHUNKS):
        back[h][slots] = jnp.zeros((vc, size), jnp.float32)
        direct[h][slots] = jnp.zeros((vc, size), jnp.float32)
    pl.semaphore_wait(barrier, len(row_offsets) + C - 1)

    def gather_copies(t, h):
        own = win[t][h].at[pl.ds(0, pt)]
        cols = [
            pltpu.make_async_remote_copy(
                src_ref=own, dst_ref=seg[t][h].at[pl.ds(c * pt, pt)],
                send_sem=col_send.at[t, h, 0, d], recv_sem=col_recv.at[t, h, 0, d],
                device_id={"col": lax.rem(c + d, C)}, device_id_type=MESH_ID)
            for d in range(1, C)
        ]
        rows = [
            pltpu.make_async_remote_copy(
                src_ref=own, dst_ref=win[t][h].at[pl.ds(b * pt, pt)],
                send_sem=row_send.at[t, h, 0, b], recv_sem=row_recv.at[t, h, 0, b],
                device_id={"row": lax.rem(r + R - b, R)}, device_id_type=MESH_ID)
            for b in range(1, half + 1)
        ]
        return cols, rows

    def row_returns(t, h):
        return [
            pltpu.make_async_remote_copy(
                src_ref=row_out[t][h].at[b - 1], dst_ref=row_in[t][h].at[b - 1],
                send_sem=row_send.at[t, h, 1, b], recv_sem=row_recv.at[t, h, 1, b],
                device_id={"row": lax.rem(r + b, R)}, device_id_type=MESH_ID)
            for b in range(1, half + 1)
        ]

    def col_returns(t, h):
        return [
            pltpu.make_async_remote_copy(
                src_ref=col_out[t][h].at[d - 1], dst_ref=col_in[t][h].at[d - 1],
                send_sem=col_send.at[t, h, 1, d], recv_sem=col_recv.at[t, h, 1, d],
                device_id={"col": lax.rem(c + d, C)}, device_id_type=MESH_ID)
            for d in range(1, C)
        ]

    started = []

    def not_far(d):
        if d == C - 1:
            return c != 0
        return c != C - 1 if d == 1 else None

    def near_far(d):
        cond = None
        if d == 2:
            cond = c == C - 2
        if d == C - 2:
            cond = c == 1 if cond is None else cond | (c == 1)
        return cond

    def when(cond, act):
        if cond is None:
            act()
        else:
            pl.when(cond)(act)

    def start_if(copy, cond):
        when(cond, copy.start)
        drains.append((copy, cond))

    drains = []

    def forward(t, h, end):
        view = seg[t][h].at[pl.ds(end * pt, pt)]
        slot = 1 if end else C - 1
        return pltpu.make_async_remote_copy(
            src_ref=view, dst_ref=view,
            send_sem=col_send.at[t, h, 2, 0], recv_sem=col_recv.at[t, h, 0, slot],
            device_id={"col": lax.rem(c + (C - 1 if end else 1), C)}, device_id_type=MESH_ID)

    def to_mid(t, h, d):
        return pltpu.make_async_remote_copy(
            src_ref=col_out[t][h].at[d - 1], dst_ref=mid[t][h],
            send_sem=col_send.at[t, h, 1, d], recv_sem=col_recv.at[t, h, 1, 0],
            device_id={"col": lax.rem(c + C - d, C)}, device_id_type=MESH_ID)

    def start_gather(t, h):
        cols, rows = gather_copies(t, h)
        for d in sorted(range(1, C), key=lambda d: -min(d, C - d)):
            start_if(cols[d - 1], not_far(d))
        return cols, start_all(rows)

    def col_sums(t, h, d, helped):
        piece = lax.rem(c + d, C)
        for j in range(pt):
            value = direct[h][last_ref[0, piece * pt + j]]
            if helped:
                value += mid[t][h][j].astype(jnp.float32)
            col_out[t][h][d - 1, j] = value.astype(jnp.bfloat16)

    def return_plain(t, h):
        copies = col_returns(t, h)
        for d in sorted(range(1, C), key=lambda d: min(d, C - d)):
            helped = near_far(d)
            plain = None if helped is None else jnp.logical_not(helped)
            when(plain, lambda: col_sums(t, h, d, False))
            straight = not_far(d)
            if straight is not None:
                start_if(to_mid(t, h, d), jnp.logical_not(straight))
            both = straight if plain is None else plain if straight is None else plain & straight
            start_if(copies[d - 1], both)
        return copies

    def return_helped(t, h):
        copies = col_returns(t, h)
        for d in range(1, C):
            helped = near_far(d)
            if helped is not None:
                def add():
                    to_mid(t, h, d).wait_recv()
                    col_sums(t, h, d, True)

                when(helped, add)
                start_if(copies[d - 1], helped)

    def start_all(copies):
        for copy in copies:
            copy.start()
        started.extend(copies)
        return copies

    def products(source, index_ref, side, sums, transposed):
        contract = (((1,), (0,)), ((), ())) if transposed else (((1,), (1,)), ((), ()))

        def one(s, carry):
            term = lax.dot_general(
                source[index_ref[0, s]], tiles[s], contract,
                preferred_element_type=jnp.float32)
            sums[s] = sums[prev_ref[side, s]] + term
            return carry

        lax.fori_loop(0, slots, one, 0, unroll=UNROLL)

    def compute(t, h, copies):
        cols, rows = copies
        for d in sorted(range(1, C), key=lambda d: -min(d, C - d)):
            cols[d - 1].wait_recv()
            if d == C - 2:
                start_if(forward(t, h, 0), c == C - 2)
            if d == 2:
                start_if(forward(t, h, C - 1), c == 1)
        if t == 0 and h == 0:
            fetch.wait()
        products(seg[t][h], rows_ref, 1, back[h], True)
        for b in range(1, half + 1):
            for j in range(pt):
                row_out[t][h][b - 1, j] = back[h][last_ref[1, b * pt + j]].astype(jnp.bfloat16)
        returns = start_all(row_returns(t, h))
        if h:
            return_helped(t, h - 1)
        for copy in rows:
            copy.wait_recv()
        products(win[t][h], cols_ref, 0, direct[h], False)
        return returns, return_plain(t, h)

    def applied(t, h, returns, j):
        total = back[h][last_ref[1, j]] + direct[h][last_ref[0, c * pt + j]]
        for b in range(half):
            total += row_in[t][h][b, j].astype(jnp.float32)
        for d in range(C - 1):
            total += col_in[t][h][d, j].astype(jnp.float32)
        return total

    shift = center_ref[0]
    width = width_ref[0]
    gathers = [None] * CHUNKS
    for h in range(CHUNKS):
        gathers[h] = start_gather(0, h)
    for t in range(2):
        returns = [compute(t, h, gathers[h]) for h in range(CHUNKS)]
        return_helped(t, CHUNKS - 1)
        for h in range(CHUNKS):
            for copy in returns[h][0]:
                copy.wait_recv()
            for d in range(1, C):
                taken = c != 0 if d == 1 else c != C - 1 if d == C - 1 else None
                when(taken, returns[h][1][d - 1].wait_recv)
            for j in range(pt):
                begin = win[0][h][j].astype(jnp.float32)
                if t == 0:
                    first = ((applied(t, h, returns, j) - shift * begin) / width).astype(jnp.bfloat16)
                    win[1][h][j] = first
                    seg[1][h][c * pt + j] = first
                else:
                    first = win[1][h][j].astype(jnp.float32)
                    value = 2.0 * (applied(t, h, returns, j) - shift * first) / width - begin
                    result[j, h * vc:(h + 1) * vc, :] = value
            if t == 0:
                gathers[h] = start_gather(1, h)
    for j in range(pt):
        out_ref[j * size:(j + 1) * size, :] = result[j].T.astype(jnp.bfloat16)
    for copy in started:
        copy.wait_send()
    for copy, cond in drains:
        when(cond, copy.wait_send)


def per_device(start_vectors, tiles, tile_rows, tile_cols, tile_counts, center, half_width):
    R = lax.axis_size("row")
    C = lax.axis_size("col")
    half = R // 2
    piece_rows, vec = start_vectors.shape
    size = tiles.shape[-1]
    slots = tiles.shape[1]
    pt = piece_rows // size
    vc = vec // CHUNKS
    row_tiles = pt * C
    col_tiles = pt * (half + 1)
    smem = pl.BlockSpec(memory_space=pltpu.SMEM)
    vmem = pl.BlockSpec(memory_space=pltpu.VMEM)
    prev, last = pl.pallas_call(
        functools.partial(link_slots, slots=slots, row_tiles=row_tiles, col_tiles=col_tiles),
        out_shape=(
            jax.ShapeDtypeStruct((2, slots), jnp.int32),
            jax.ShapeDtypeStruct((2, max(row_tiles, col_tiles)), jnp.int32),
        ),
        in_specs=[smem] * 3,
        out_specs=(smem, smem),
        name="link_slots",
    )(tile_rows, tile_cols, tile_counts)

    bf, f32 = jnp.bfloat16, jnp.float32

    def pair(shape, dtype):
        return [pltpu.VMEM(shape, dtype) for _ in range(2 * CHUNKS)]

    scratch = (
        pair((col_tiles, vc, size), bf)
        + pair((row_tiles, vc, size), bf)
        + pair((half, pt, vc, size), bf)
        + pair((C - 1, pt, vc, size), bf)
        + pair((half, pt, vc, size), bf)
        + pair((C - 1, pt, vc, size), bf)
        + [pltpu.VMEM((slots + 1, vc, size), f32) for _ in range(2 * CHUNKS)]
        + pair((pt, vc, size), bf)
        + [pltpu.VMEM((pt, vec, size), f32), pltpu.VMEM((slots, size, size), bf), pltpu.SemaphoreType.DMA]
        + [pltpu.SemaphoreType.DMA((2, CHUNKS, 2, half + 1))] * 2
        + [pltpu.SemaphoreType.DMA((2, CHUNKS, 3, C))] * 2
    )
    return pl.pallas_call(
        functools.partial(filter_kernel, (R, C, half, pt, slots, vec, size)),
        out_shape=jax.ShapeDtypeStruct((piece_rows, vec), bf),
        in_specs=[vmem, pl.BlockSpec(memory_space=pl.ANY), smem, smem, smem, smem, smem, smem],
        out_specs=vmem,
        scratch_shapes=scratch,
        compiler_params=pltpu.CompilerParams(
            collective_id=0, has_side_effects=True, vmem_limit_bytes=40 << 20),
        name="filter_steps",
    )(start_vectors, tiles, tile_rows, tile_cols, prev, last, center, half_width)


def solution(mesh):
    return jax.shard_map(
        per_device,
        mesh=mesh,
        in_specs=(
            P(("row", "col"), None),
            P("row", "col", None, None),
            P("row", "col"),
            P("row", "col"),
            P("row", "col"),
            P(),
            P(),
        ),
        out_specs=P(("row", "col"), None),
        check_vma=False,
    )
```

```python
import functools

import jax
import jax.numpy as jnp
from jax import lax
from jax.experimental import pallas as pl
from jax.experimental.pallas import tpu as pltpu
from jax.sharding import PartitionSpec as P

CHUNKS = 2
UNROLL = 16
MESH_ID = pl.DeviceIdType.MESH


def link_slots(rows_ref, cols_ref, counts_ref, prev_ref, last_ref, *, slots, row_tiles, col_tiles):
    for side, (keys, size) in enumerate(((rows_ref, row_tiles), (cols_ref, col_tiles))):
        for k in range(size):
            last_ref[side, k] = slots
        for s in range(slots):
            key = keys[0, s]
            used = s < counts_ref[0, 0]
            before = last_ref[side, key]
            prev_ref[side, s] = jnp.where(used, before, slots)
            last_ref[side, key] = jnp.where(used, s, before)


def filter_kernel(
    dims, x_ref, tiles_ref, rows_ref, cols_ref, prev_ref, last_ref, center_ref, width_ref,
    out_ref, *scratch,
):
    R, C, half, pt, slots, vec, size = dims
    vc = vec // CHUNKS
    it = iter(scratch)
    win = [[next(it) for _ in range(CHUNKS)] for _ in range(2)]
    seg = [[next(it) for _ in range(CHUNKS)] for _ in range(2)]
    row_out = [[next(it) for _ in range(CHUNKS)] for _ in range(2)]
    col_out = [[next(it) for _ in range(CHUNKS)] for _ in range(2)]
    row_in = [[next(it) for _ in range(CHUNKS)] for _ in range(2)]
    col_in = [[next(it) for _ in range(CHUNKS)] for _ in range(2)]
    back = [next(it) for _ in range(CHUNKS)]
    direct = [next(it) for _ in range(CHUNKS)]
    mid = [[next(it) for _ in range(CHUNKS)] for _ in range(2)]
    result = next(it)
    tiles, local = next(it), next(it)
    row_send, row_recv, col_send, col_recv = (next(it) for _ in range(4))

    r = lax.axis_index("row")
    c = lax.axis_index("col")

    row_offsets = sorted({b % R for b in range(1, half + 1)} | {-b % R for b in range(1, half + 1)})
    barrier = pltpu.get_barrier_semaphore()
    for off in row_offsets:
        pl.semaphore_signal(barrier, inc=1, device_id={"row": lax.rem(r + off, R)}, device_id_type=MESH_ID)
    for off in range(1, C):
        pl.semaphore_signal(barrier, inc=1, device_id={"col": lax.rem(c + off, C)}, device_id_type=MESH_ID)

    fetch = pltpu.make_async_copy(tiles_ref.at[0], tiles, local)
    fetch.start()
    for end, slot in ((0, 0), (C - 1, C - 2)):
        @pl.when(c == end)
        def _():
            for t in range(2):
                for h in range(CHUNKS):
                    col_in[t][h][slot] = jnp.zeros((pt, vc, size), jnp.bfloat16)
    for j in range(pt):
        block = x_ref[j * size:(j + 1) * size, :].astype(jnp.float32).T.astype(jnp.bfloat16)
        for h in range(CHUNKS):
            part = block[h * vc:(h + 1) * vc, :]
            win[0][h][j] = part
            seg[0][h][c * pt + j] = part
    for h in range(CHUNKS):
        back[h][slots] = jnp.zeros((vc, size), jnp.float32)
        direct[h][slots] = jnp.zeros((vc, size), jnp.float32)
    pl.semaphore_wait(barrier, len(row_offsets) + C - 1)

    def gather_copies(t, h):
        own = win[t][h].at[pl.ds(0, pt)]
        cols = [
            pltpu.make_async_remote_copy(
                src_ref=own, dst_ref=seg[t][h].at[pl.ds(c * pt, pt)],
                send_sem=col_send.at[t, h, 0, d], recv_sem=col_recv.at[t, h, 0, d],
                device_id={"col": lax.rem(c + d, C)}, device_id_type=MESH_ID)
            for d in range(1, C)
        ]
        rows = [
            pltpu.make_async_remote_copy(
                src_ref=own, dst_ref=win[t][h].at[pl.ds(b * pt, pt)],
                send_sem=row_send.at[t, h, 0, b], recv_sem=row_recv.at[t, h, 0, b],
                device_id={"row": lax.rem(r + R - b, R)}, device_id_type=MESH_ID)
            for b in range(1, half + 1)
        ]
        return cols, rows

    def row_returns(t, h):
        return [
            pltpu.make_async_remote_copy(
                src_ref=row_out[t][h].at[b - 1], dst_ref=row_in[t][h].at[b - 1],
                send_sem=row_send.at[t, h, 1, b], recv_sem=row_recv.at[t, h, 1, b],
                device_id={"row": lax.rem(r + b, R)}, device_id_type=MESH_ID)
            for b in range(1, half + 1)
        ]

    def col_returns(t, h):
        return [
            pltpu.make_async_remote_copy(
                src_ref=col_out[t][h].at[d - 1], dst_ref=col_in[t][h].at[d - 1],
                send_sem=col_send.at[t, h, 1, d], recv_sem=col_recv.at[t, h, 1, d],
                device_id={"col": lax.rem(c + d, C)}, device_id_type=MESH_ID)
            for d in range(1, C)
        ]

    started = []

    def not_far(d):
        if d == C - 1:
            return c != 0
        return c != C - 1 if d == 1 else None

    def near_far(d):
        cond = None
        if d == 2:
            cond = c == C - 2
        if d == C - 2:
            cond = c == 1 if cond is None else cond | (c == 1)
        return cond

    def when(cond, act):
        if cond is None:
            act()
        else:
            pl.when(cond)(act)

    def start_if(copy, cond):
        when(cond, copy.start)
        drains.append((copy, cond))

    drains = []

    def forward(t, h, end):
        view = seg[t][h].at[pl.ds(end * pt, pt)]
        slot = 1 if end else C - 1
        return pltpu.make_async_remote_copy(
            src_ref=view, dst_ref=view,
            send_sem=col_send.at[t, h, 2, 0], recv_sem=col_recv.at[t, h, 0, slot],
            device_id={"col": lax.rem(c + (C - 1 if end else 1), C)}, device_id_type=MESH_ID)

    def to_mid(t, h, d):
        return pltpu.make_async_remote_copy(
            src_ref=col_out[t][h].at[d - 1], dst_ref=mid[t][h],
            send_sem=col_send.at[t, h, 1, d], recv_sem=col_recv.at[t, h, 1, 0],
            device_id={"col": lax.rem(c + C - d, C)}, device_id_type=MESH_ID)

    def start_gather(t, h):
        cols, rows = gather_copies(t, h)
        for d in sorted(range(1, C), key=lambda d: -min(d, C - d)):
            start_if(cols[d - 1], not_far(d))
        return cols, start_all(rows)

    def col_sums(t, h, d, helped):
        piece = lax.rem(c + d, C)
        for j in range(pt):
            value = direct[h][last_ref[0, piece * pt + j]]
            if helped:
                value += mid[t][h][j].astype(jnp.float32)
            col_out[t][h][d - 1, j] = value.astype(jnp.bfloat16)

    def return_plain(t, h):
        copies = col_returns(t, h)
        for d in sorted(range(1, C), key=lambda d: min(d, C - d)):
            helped = near_far(d)
            plain = None if helped is None else jnp.logical_not(helped)
            when(plain, lambda: col_sums(t, h, d, False))
            straight = not_far(d)
            if straight is not None:
                start_if(to_mid(t, h, d), jnp.logical_not(straight))
            both = straight if plain is None else plain if straight is None else plain & straight
            start_if(copies[d - 1], both)
        return copies

    def return_helped(t, h):
        copies = col_returns(t, h)
        for d in range(1, C):
            helped = near_far(d)
            if helped is not None:
                def add():
                    to_mid(t, h, d).wait_recv()
                    col_sums(t, h, d, True)

                when(helped, add)
                start_if(copies[d - 1], helped)

    def start_all(copies):
        for copy in copies:
            copy.start()
        started.extend(copies)
        return copies

    def products(source, index_ref, side, sums, transposed):
        contract = (((1,), (0,)), ((), ())) if transposed else (((1,), (1,)), ((), ()))

        def one(s, carry):
            term = lax.dot_general(
                source[index_ref[0, s]], tiles[s], contract,
                preferred_element_type=jnp.float32)
            sums[s] = sums[prev_ref[side, s]] + term
            return carry

        lax.fori_loop(0, slots, one, 0, unroll=UNROLL)

    def compute(t, h, copies):
        cols, rows = copies
        for d in sorted(range(1, C), key=lambda d: -min(d, C - d)):
            cols[d - 1].wait_recv()
            if d == C - 2:
                start_if(forward(t, h, 0), c == C - 2)
            if d == 2:
                start_if(forward(t, h, C - 1), c == 1)
        if t == 0 and h == 0:
            fetch.wait()
        products(seg[t][h], rows_ref, 1, back[h], True)
        for b in range(1, half + 1):
            for j in range(pt):
                row_out[t][h][b - 1, j] = back[h][last_ref[1, b * pt + j]].astype(jnp.bfloat16)
        returns = start_all(row_returns(t, h))
        if h:
            return_helped(t, h - 1)
        for copy in rows:
            copy.wait_recv()
        products(win[t][h], cols_ref, 0, direct[h], False)
        return returns, return_plain(t, h)

    def applied(t, h, returns, j):
        total = back[h][last_ref[1, j]] + direct[h][last_ref[0, c * pt + j]]
        for b in range(half):
            total += row_in[t][h][b, j].astype(jnp.float32)
        for d in range(C - 1):
            total += col_in[t][h][d, j].astype(jnp.float32)
        return total

    shift = center_ref[0]
    width = width_ref[0]
    gathers = [None] * CHUNKS
    for h in range(CHUNKS):
        gathers[h] = start_gather(0, h)
    for t in range(2):
        returns = [compute(t, h, gathers[h]) for h in range(CHUNKS)]
        return_helped(t, CHUNKS - 1)
        for h in range(CHUNKS):
            for copy in returns[h][0]:
                copy.wait_recv()
            for d in range(1, C):
                taken = c != 0 if d == 1 else c != C - 1 if d == C - 1 else None
                when(taken, returns[h][1][d - 1].wait_recv)
            for j in range(pt):
                begin = win[0][h][j].astype(jnp.float32)
                if t == 0:
                    first = ((applied(t, h, returns, j) - shift * begin) / width).astype(jnp.bfloat16)
                    win[1][h][j] = first
                    seg[1][h][c * pt + j] = first
                else:
                    first = win[1][h][j].astype(jnp.float32)
                    value = 2.0 * (applied(t, h, returns, j) - shift * first) / width - begin
                    result[j, h * vc:(h + 1) * vc, :] = value
            if t == 0:
                gathers[h] = start_gather(1, h)
    for j in range(pt):
        out_ref[j * size:(j + 1) * size, :] = result[j].T.astype(jnp.bfloat16)
    for copy in started:
        copy.wait_send()
    for copy, cond in drains:
        when(cond, copy.wait_send)


def per_device(start_vectors, tiles, tile_rows, tile_cols, tile_counts, center, half_width):
    R = lax.axis_size("row")
    C = lax.axis_size("col")
    half = R // 2
    piece_rows, vec = start_vectors.shape
    size = tiles.shape[-1]
    slots = tiles.shape[1]
    pt = piece_rows // size
    vc = vec // CHUNKS
    row_tiles = pt * C
    col_tiles = pt * (half + 1)
    smem = pl.BlockSpec(memory_space=pltpu.SMEM)
    vmem = pl.BlockSpec(memory_space=pltpu.VMEM)
    prev, last = pl.pallas_call(
        functools.partial(link_slots, slots=slots, row_tiles=row_tiles, col_tiles=col_tiles),
        out_shape=(
            jax.ShapeDtypeStruct((2, slots), jnp.int32),
            jax.ShapeDtypeStruct((2, max(row_tiles, col_tiles)), jnp.int32),
        ),
        in_specs=[smem] * 3,
        out_specs=(smem, smem),
        name="link_slots",
    )(tile_rows, tile_cols, tile_counts)

    bf, f32 = jnp.bfloat16, jnp.float32

    def pair(shape, dtype):
        return [pltpu.VMEM(shape, dtype) for _ in range(2 * CHUNKS)]

    scratch = (
        pair((col_tiles, vc, size), bf)
        + pair((row_tiles, vc, size), bf)
        + pair((half, pt, vc, size), bf)
        + pair((C - 1, pt, vc, size), bf)
        + pair((half, pt, vc, size), bf)
        + pair((C - 1, pt, vc, size), bf)
        + [pltpu.VMEM((slots + 1, vc, size), f32) for _ in range(2 * CHUNKS)]
        + pair((pt, vc, size), bf)
        + [pltpu.VMEM((pt, vec, size), f32), pltpu.VMEM((slots, size, size), bf), pltpu.SemaphoreType.DMA]
        + [pltpu.SemaphoreType.DMA((2, CHUNKS, 2, half + 1))] * 2
        + [pltpu.SemaphoreType.DMA((2, CHUNKS, 3, C))] * 2
    )
    return pl.pallas_call(
        functools.partial(filter_kernel, (R, C, half, pt, slots, vec, size)),
        out_shape=jax.ShapeDtypeStruct((piece_rows, vec), bf),
        in_specs=[vmem, pl.BlockSpec(memory_space=pl.ANY), smem, smem, smem, smem, smem, smem],
        out_specs=vmem,
        scratch_shapes=scratch,
        compiler_params=pltpu.CompilerParams(
            collective_id=0, has_side_effects=True, vmem_limit_bytes=40 << 20),
        name="filter_steps",
    )(start_vectors, tiles, tile_rows, tile_cols, prev, last, center, half_width)


def solution(mesh):
    return jax.shard_map(
        per_device,
        mesh=mesh,
        in_specs=(
            P(("row", "col"), None),
            P("row", "col", None, None),
            P("row", "col"),
            P("row", "col"),
            P("row", "col"),
            P(),
            P(),
        ),
        out_specs=P(("row", "col"), None),
        check_vma=False,
    )
```
